32 devices in a mesh: dp: 16 (over z, x, core), seq: 2 (over y).
Axes of the slice: x: 2, y: 2, z: 4, core: 2. Of those that a mesh axis runs over, the one named last changes fastest.
Arguments:
- layer_input: bfloat16 [2, 16, 1024, 1024], P(None, 'dp', 'seq'), may hold values from -6 to 6
- lengths: int32 [2, 16], P(None, 'dp'), may hold values from 512 to 1024, as said below
- out_grad: bfloat16 [2, 16, 1024, 1024], P(None, 'dp', 'seq'), may hold values from -6 to 6
- ln1_gain: bfloat16 [1024], P(('dp', 'seq')), may hold values from 0.5 to 1.5
- ln1_shift: bfloat16 [1024], P(('dp', 'seq')), may hold values from -1 to 1
- w_qkv: bfloat16 [1024, 3072], P(('dp', 'seq')), may hold values from -0.1875 to 0.1875
- b_query: bfloat16 [1024], P(('dp', 'seq')), may hold values from -1.5 to 1.5
- b_value: bfloat16 [1024], P(('dp', 'seq')), may hold values from -1.5 to 1.5
- w_out: bfloat16 [1024, 1024], P(('dp', 'seq')), may hold values from -1.5 to 1.5
- b_out: bfloat16 [1024], P(('dp', 'seq')), may hold values from -1 to 1
- ln2_gain: bfloat16 [1024], P(('dp', 'seq')), may hold values from 0.5 to 1.5
- ln2_shift: bfloat16 [1024], P(('dp', 'seq')), may hold values from -1 to 1
- w_in: bfloat16 [1024, 4096], P(('dp', 'seq')), may hold values from -0.1875 to 0.1875
- b_in: bfloat16 [4096], P(('dp', 'seq')), may hold values from -1 to 1
- w_down: bfloat16 [4096, 1024], P(('dp', 'seq')), may hold values from -0.09375 to 0.09375
- b_down: bfloat16 [1024], P(('dp', 'seq')), may hold values from -1 to 1
Outputs:
- out: bfloat16 [2, 16, 1024, 1024], P(None, 'dp', 'seq')
- x_grad: bfloat16 [2, 16, 1024, 1024], P(None, 'dp', 'seq')
- grad_ln1_gain: float32 [1024], P(('dp', 'seq'))
- grad_ln1_shift: float32 [1024], P(('dp', 'seq'))
- grad_w_qkv: float32 [1024, 3072], P(('dp', 'seq'))
- grad_b_query: float32 [1024], P(('dp', 'seq'))
- grad_b_value: float32 [1024], P(('dp', 'seq'))
- grad_w_out: float32 [1024, 1024], P(('dp', 'seq'))
- grad_b_out: float32 [1024], P(('dp', 'seq'))
- grad_ln2_gain: float32 [1024], P(('dp', 'seq'))
- grad_ln2_shift: float32 [1024], P(('dp', 'seq'))
- grad_w_in: float32 [1024, 4096], P(('dp', 'seq'))
- grad_b_in: float32 [4096], P(('dp', 'seq'))
- grad_w_down: float32 [4096, 1024], P(('dp', 'seq'))
- grad_b_down: float32 [1024], P(('dp', 'seq'))
The draws below stay inside these ranges and needn't reach their ends.
Inputs may be any that keep to these rules, and one draw needn't show every extreme that they name: `lengths`: slots at or beyond a sequence's length are padding; one sequence has length 1024 and one 1024 // 2 in every draw.
All inputs are finite; a program needn't handle non-finite values.
Results may differ from the reference program's by a relative error of at most 0.011.
Values may be sent and summed in bfloat16 or wider, within the bound.
No kernel may reach another device: no remote copies, remote signals or barrier semaphores. Data moves between devices by JAX's collectives and lax.ppermute only.
A program may use at most 136 MiB of HBM per device.

```python
import jax
import jax.numpy as jnp
from jax import lax

D = 1024
HD = 64
FF = 4096
S = 1024
MB = 2
BATCH = 16


def draw_lengths(key, part):
    drawn = jax.random.randint(key, (MB, BATCH), S // 2, S + 1)
    place = jnp.arange(MB * BATCH).reshape(MB, BATCH)
    drawn = jnp.where(place == 0, S, drawn)
    drawn = jnp.where(place == 1, S // 2, drawn)
    return drawn.astype(jnp.int32)


def spiked(values, stream_key, source, target, parts, factor):
    owner, partner = [(jnp.arange(values.shape[position]) // (values.shape[position] // parts)).reshape([-1 if axis == position else 1 for axis in range(values.ndim)]) for position in (source, target)]
    chosen = jax.random.permutation(stream_key, parts)[partner]
    strong = (owner == chosen) | (owner == (partner + parts // 2) % parts)
    return jnp.where(strong, factor * values, values)


def level_of(rng, dims, split, least, top_value):
    level, own = 1.0, jax.random.fold_in(rng, 6)
    for axis_at, parts in split:
        draws = jnp.exp(jax.random.uniform(jax.random.fold_in(own, axis_at), (parts,), jnp.float32, least / len(split), top_value / len(split)))
        level = level * jnp.repeat(draws, dims[axis_at] // parts).reshape([-1 if axis == axis_at else 1 for axis in range(len(dims))])
    return level


def centred(own_key, shape, scale, limit, cuts=(), kind=jnp.bfloat16):
    array = scale * jax.random.normal(own_key, shape, jnp.float32)
    if cuts:
        array = array * level_of(own_key, shape, cuts, -0.22, 0.18)
    return jnp.clip(array, -limit, limit).astype(kind)


def gaussian_with(rng, shape, scale, most, split, heavy, kind=jnp.bfloat16):
    values = scale * jax.random.normal(rng, shape, jnp.float32)
    if split:
        values = values * level_of(rng, shape, split, -0.22, 0.18)
    return jnp.clip(spiked(values, jax.random.fold_in(rng, 3), *heavy), -most, most).astype(kind)


def setup_inputs(seed: int = 0) -> dict:
    splits = jax.random.split(jax.random.key(seed), 17)
    return {
        "layer_input": gaussian_with(splits[0], (MB, BATCH, S, D), 1.0, 6.0, ((1, 16), (2, 2)), (1, 3, 16, 2.0)),
        "lengths": draw_lengths(jax.random.fold_in(splits[16], 71), 0),
        "out_grad": centred(splits[2], (MB, BATCH, S, D), 1.0, 6.0, ((1, 16), (2, 2))),
        "ln1_gain": jnp.clip(1.0 + 0.1 * jax.random.normal(splits[3], (D,), jnp.float32), 0.5, 1.5).astype(jnp.bfloat16),
        "ln1_shift": centred(splits[4], (D,), 0.2, 1.0, ((0, 32),)),
        "w_qkv": centred(splits[5], (D, 3 * D), D ** -0.5, 0.1875, ((0, 32),)),
        "b_query": centred(splits[6], (D,), 0.3, 1.5, ((0, 32),)),
        "b_value": centred(splits[7], (D,), 0.3, 1.5, ((0, 32),)),
        "w_out": centred(splits[8], (D, D), (D // 64) ** -0.5, 1.5, ((0, 32),)),
        "b_out": centred(splits[9], (D,), 0.2, 1.0, ((0, 32),)),
        "ln2_gain": jnp.clip(1.0 + 0.1 * jax.random.normal(splits[10], (D,), jnp.float32), 0.5, 1.5).astype(jnp.bfloat16),
        "ln2_shift": centred(splits[11], (D,), 0.2, 1.0, ((0, 32),)),
        "w_in": centred(splits[12], (D, FF), D ** -0.5, 0.1875, ((0, 32),)),
        "b_in": centred(splits[13], (FF,), 0.2, 1.0, ((0, 32),)),
        "w_down": centred(splits[14], (FF, D), FF ** -0.5, 0.09375, ((0, 32),)),
        "b_down": centred(splits[15], (D,), 0.2, 1.0, ((0, 32),)),
    }


EPSILON = 1e-05

@jax.custom_vjp
def low(v):
    return lax.optimization_barrier(v.astype(jnp.bfloat16)).astype(jnp.float32)

@jax.custom_vjp
def low_back(v):
    return v

def low_keep(v):
    return (low(v), None)

def low_pass(kept, grad):
    return (grad,)

def back_keep(v):
    return (v, None)

def back_low(kept, grad):
    return (low(grad),)
low.defvjp(low_keep, low_pass)
low_back.defvjp(back_keep, back_low)

def matmul(left, right):
    return jnp.dot(left, right, precision=lax.Precision.HIGHEST)

def layer_norm(values, gain, shift):
    center = values - lax.optimization_barrier(jnp.mean(values, axis=-1, keepdims=True))
    spread = lax.optimization_barrier(jnp.mean(center * center, axis=-1, keepdims=True))
    return center * lax.rsqrt(spread + EPSILON) * gain + shift

def gelu_tanh(values):
    return 0.5 * values * (1.0 + jnp.tanh(0.7978845608028654 * (values + 0.044715 * values * values * values)))

def split_heads(rows):
    count = rows.shape[0]
    heads = rows.shape[1] // HD
    return rows.reshape(count, heads, HD).transpose(1, 0, 2)

def forward(params, inputs, length):
    ln1_gain, ln1_shift, w_qkv, b_query, b_value, w_out, b_out, ln2_gain, ln2_shift, w_in, b_in, w_down, b_down = params
    width = inputs.shape[1]
    count = inputs.shape[0]
    slots = jnp.arange(count, dtype=jnp.int32)
    live = (slots < length).astype(jnp.float32)[:, None]
    normed = low(layer_norm(inputs, ln1_gain, ln1_shift))
    joined = matmul(normed, w_qkv)
    query = low(low_back(joined[:, :width] + b_query))
    keys = low(low_back(joined[:, width:2 * width]))
    values = low(low_back(joined[:, 2 * width:] + b_value))
    scores = jnp.einsum('hqd,hkd->hqk', split_heads(query), split_heads(keys), precision=lax.Precision.HIGHEST) * HD ** (-0.5)
    scores = low_back(scores)
    allowed = (slots[None, :] <= slots[:, None]) & (slots[None, :] < length)
    scores = jnp.where(allowed[None], scores, -1e+30)
    probs = low(jax.nn.softmax(scores, axis=-1))
    mixed = jnp.einsum('hqk,hkd->hqd', probs, split_heads(values), precision=lax.Precision.HIGHEST)
    mixed = low(low_back(mixed.transpose(1, 0, 2).reshape(count, width)))
    attended = low_back(matmul(mixed, w_out) + b_out)
    middle = inputs + attended
    hidden_in = low(layer_norm(middle, ln2_gain, ln2_shift))
    before = low_back(matmul(hidden_in, w_in) + b_in)
    activated = low(gelu_tanh(before))
    branch = low_back(matmul(activated, w_down) + b_down)
    return live * (middle + branch)

def reference(layer_input, lengths, out_grad, ln1_gain, ln1_shift, w_qkv, b_query, b_value, w_out, b_out, ln2_gain, ln2_shift, w_in, b_in, w_down, b_down):
    params = (ln1_gain, ln1_shift, w_qkv, b_query, b_value, w_out, b_out, ln2_gain, ln2_shift, w_in, b_in, w_down, b_down)
    params = tuple((piece.astype(jnp.float32) for piece in params))
    samples = layer_input.reshape(MB * BATCH, S, D)
    cotangents = out_grad.reshape(MB * BATCH, S, D)
    spans = lengths.reshape(MB * BATCH).astype(jnp.int32)
    zeros = tuple((jnp.zeros_like(piece) for piece in params))

    def visit(totals, item):
        sample, length, cotangent = item

        def apply(weights, values):
            return forward(weights, values, length)
        result, pull = jax.vjp(apply, params, sample.astype(jnp.float32))
        weight_grads, input_grad = pull(cotangent.astype(jnp.float32))
        totals = tuple((first + second for first, second in zip(totals, weight_grads)))
        return (totals, (result.astype(jnp.bfloat16), input_grad.astype(jnp.bfloat16)))
    totals, stacked = lax.scan(visit, zeros, (samples, spans, cotangents))
    outputs = stacked[0].reshape(layer_input.shape)
    input_grads = stacked[1].reshape(layer_input.shape)
    return (outputs, input_grads, totals[0], totals[1], totals[2], totals[3], totals[4], totals[5], totals[6], totals[7], totals[8], totals[9], totals[10], totals[11], totals[12])
```

```python
import functools

import jax
import jax.numpy as jnp
from jax import lax
from jax.experimental import pallas as pl
from jax.experimental.pallas import tpu as pltpu
from jax.sharding import PartitionSpec as P

HD = 64
EPSILON = 1e-05
LANES = 128
LOW = jnp.bfloat16
F32 = jnp.float32
MASKED = -1e30


def box():
    devices = lax.axis_size("dp")
    rest = devices // 4
    index = lax.axis_index("dp")
    return {
        "z": rest,
        "zi": index // 4,
        "xi": (index // 2) % 2,
        "ci": index % 2,
        "yi": lax.axis_index("seq"),
    }


def swap(value, name):
    if name == "y":
        return lax.ppermute(value, "seq", [(0, 1), (1, 0)])
    bit = {"x": 2, "c": 1}[name]
    return lax.ppermute(value, "dp", [(i, i ^ bit) for i in range(lax.axis_size("dp"))])


def next_z(value):
    devices = lax.axis_size("dp")
    return lax.ppermute(value, "dp", [(i, (i + 4) % devices) for i in range(devices)])


def pick(value, index, axis):
    return lax.dynamic_index_in_dim(value, index, axis, keepdims=False)


def ordered(own, other, index, axis):
    triple = jnp.stack([own, other, own], axis=axis)
    return lax.dynamic_slice_in_dim(triple, index, 2, axis)


def gather_z(shard, place):
    chain = [shard]
    for _ in range(place["z"] - 1):
        chain.append(next_z(chain[-1]))
    line = jnp.stack(chain[::-1] + chain[:0:-1], axis=0)
    return lax.dynamic_slice_in_dim(line, place["z"] - 1 - place["zi"], place["z"], 0)


def gather_rest(part, order, place):
    if order == "xy":
        part = ordered(part, swap(part, "x"), place["xi"], 1)
        part = ordered(part, swap(part, "y"), place["yi"], 2)
    else:
        part = ordered(part, swap(part, "y"), place["yi"], 1)
        part = ordered(part, swap(part, "x"), place["xi"], 1)
    return ordered(part, swap(part, "c"), place["ci"], 2)


def whole(part):
    return part.reshape(-1, part.shape[-1])


def halve(value, name, index, axis):
    other = swap(pick(value, 1 - index, axis), name)
    return (pick(value, index, axis).astype(F32) + other.astype(F32)).astype(LOW)


def scatter_core(total, place):
    rest, rows = place["z"], total.shape[0]
    parts = rest * 8
    value = total.reshape(rest, 2, 2, 2, rows // parts, total.shape[1])
    return halve(value, "c", place["ci"], 2)


def scatter_xy(value, order, place):
    if order == "yx":
        value = halve(value, "y", place["yi"], 2)
        return halve(value, "x", place["xi"], 1)
    value = halve(value, "x", place["xi"], 1)
    return halve(value, "y", place["yi"], 1)


def scatter_z(value, place):
    rest = place["z"]
    carried = None
    for step in range(1, rest):
        mine = pick(value, (place["zi"] - step) % rest, 0)
        if carried is not None:
            mine = (mine.astype(F32) + carried.astype(F32)).astype(LOW)
        carried = next_z(mine)
    return pick(value, place["zi"], 0).astype(F32) + carried.astype(F32)


def nt(left, right):
    return lax.dot_general(left, right, (((1,), (1,)), ((), ())), preferred_element_type=F32)


def nn(left, right):
    return jnp.dot(left, right, preferred_element_type=F32)


def head_lanes(rows, head):
    lane = lax.broadcasted_iota(jnp.int32, (rows, LANES), 1)
    return (lane < HD) if head == 0 else (lane >= HD)


def attend_kernel(info, q_ref, k_ref, v_ref, mixed_ref, lse_ref, bias_ref):
    batch = pl.program_id(0)
    slots = q_ref.shape[0]
    half = slots // 2

    @pl.when(pl.program_id(1) == 0)
    def _():
        rows = lax.broadcasted_iota(jnp.int32, (slots, slots), 0)
        cols = lax.broadcasted_iota(jnp.int32, (slots, slots), 1)
        allowed = (cols <= rows) & (cols < info[1 + batch])
        bias_ref[...] = jnp.where(allowed, 0.0, MASKED)

    def run(early):
        for block in range(2):
            rows = pl.ds(block * half, half)
            q = q_ref[rows, :] * LOW(0.125)
            span = half * (block + 1)
            outs = []
            for head in range(2):
                mine = jnp.where(head_lanes(half, head), q, LOW(0))
                late = nt(mine, k_ref[slots : slots + span, :]) + bias_ref[rows, :span]
                peak = jnp.max(late, axis=1, keepdims=True)
                if early:
                    first = nt(mine, k_ref[:slots, :])
                    peak = jnp.maximum(peak, jnp.max(first, axis=1, keepdims=True))
                late = jnp.exp(late - peak)
                total = jnp.sum(late, axis=1, keepdims=True)
                out = nn(late.astype(LOW), v_ref[slots : slots + span, :])
                if early:
                    first = jnp.exp(first - peak)
                    total = total + jnp.sum(first, axis=1, keepdims=True)
                    out = out + nn(first.astype(LOW), v_ref[:slots, :])
                outs.append(out / total)
                lse = jnp.broadcast_to(peak + jnp.log(total), (half, LANES))
                lse_ref[0, 0, head : head + 1, rows] = lse.T[:1, :]
            mixed_ref[rows, :] = jnp.where(head_lanes(half, 0), outs[0], outs[1]).astype(LOW)

    @pl.when(info[0] == 0)
    def _():
        run(False)

    @pl.when(info[0] != 0)
    def _():
        run(True)


def attend(info, query, joined):
    tokens, width = query.shape
    batches = info.shape[0] - 1
    slots = tokens // batches
    pairs = width // LANES
    spec = lambda rows, place: pl.BlockSpec((rows, LANES), place)
    return pl.pallas_call(
        attend_kernel,
        out_shape=(
            jax.ShapeDtypeStruct((tokens, width), LOW),
            jax.ShapeDtypeStruct((batches, pairs, 8, slots), F32),
        ),
        grid_spec=pltpu.PrefetchScalarGridSpec(
            num_scalar_prefetch=1,
            grid=(batches, pairs),
            in_specs=[
                spec(slots, lambda b, h, info: (b, h)),
                spec(2 * slots, lambda b, h, info: (b, h)),
                spec(2 * slots, lambda b, h, info: (b, h + pairs)),
            ],
            out_specs=[
                spec(slots, lambda b, h, info: (b, h)),
                pl.BlockSpec((1, 1, 8, slots), lambda b, h, info: (b, h, 0, 0)),
            ],
            scratch_shapes=[pltpu.VMEM((slots, slots), F32)],
        ),
        cost_estimate=pl.CostEstimate(
            flops=batches * pairs * 8 * slots * slots * 7 * HD,
            bytes_accessed=12 * tokens * width,
            transcendentals=batches * pairs * 4 * slots * slots,
        ),
        name="attend",
    )(info, query, joined, joined)


def attend_back_kernel(
    info, q_ref, k_ref, v_ref, g_ref, mixed_ref, lse_ref, dq_ref, dk_ref, dv_ref, bias_ref
):
    batch = pl.program_id(0)
    slots = q_ref.shape[0]
    half = slots // 2

    @pl.when(pl.program_id(1) == 0)
    def _():
        keys = lax.broadcasted_iota(jnp.int32, (slots, slots), 0)
        rows = lax.broadcasted_iota(jnp.int32, (slots, slots), 1)
        allowed = (keys <= rows) & (keys < info[1 + batch])
        bias_ref[...] = jnp.where(allowed, 0.0, MASKED)

    def run(early):
        q = q_ref[...] * LOW(0.125)
        g = g_ref[...]
        inner = (g.astype(F32) * mixed_ref[...].astype(F32)).T
        keys_turned = k_ref[...].T
        qs, gs, inners, lses, sums = [], [], [], [], []
        for head in range(2):
            lanes = head_lanes(slots, head)
            qs.append(jnp.where(lanes, q, LOW(0)))
            gs.append(jnp.where(lanes, g, LOW(0)))
            inners.append(jnp.sum(inner[head * HD : (head + 1) * HD], axis=0, keepdims=True))
            lses.append(lse_ref[0, 0, head : head + 1, :])
            sums.append([None, None])
        for chunk in range(0 if early else 2, 4):
            keys = slice(chunk * half, (chunk + 1) * half)
            first = 1 if chunk == 3 else 0
            live = slice(first * half, slots)
            k, v = k_ref[keys, :], v_ref[keys, :]
            dk = dv = None
            for head in range(2):
                score = nt(k, qs[head][live])
                if chunk >= 2:
                    score = score + bias_ref[(chunk - 2) * half : (chunk - 1) * half, live]
                prob = jnp.exp(score - lses[head][:, live])
                grad_prob = nt(v, gs[head][live])
                grad = (prob * (grad_prob - inners[head][:, live])).astype(LOW)
                one = nn(prob.astype(LOW), gs[head][live])
                two = nn(grad, qs[head][live])
                dv = one if dv is None else dv + one
                dk = two if dk is None else dk + two
                turned = nn(keys_turned[head * HD : (head + 1) * HD, keys], grad)
                for block in range(first, 2):
                    piece = turned[:, (block - first) * half : (block - first + 1) * half]
                    old = sums[head][block]
                    sums[head][block] = piece if old is None else old + piece
            dk_ref[keys, :] = dk.astype(LOW)
            dv_ref[keys, :] = dv.astype(LOW)
        for block in range(2):
            both = jnp.concatenate([sums[0][block], sums[1][block]], axis=0)
            dq_ref[block * half : (block + 1) * half, :] = (both.T * 0.125).astype(LOW)
        if not early:
            dk_ref[:slots, :] = jnp.zeros((slots, LANES), LOW)
            dv_ref[:slots, :] = jnp.zeros((slots, LANES), LOW)

    @pl.when(info[0] == 0)
    def _():
        run(False)

    @pl.when(info[0] != 0)
    def _():
        run(True)


def attend_back(info, query, joined, grad, mixed, lse):
    tokens, width = query.shape
    batches = info.shape[0] - 1
    slots = tokens // batches
    pairs = width // LANES
    spec = lambda rows, place: pl.BlockSpec((rows, LANES), place)
    here = lambda b, h, info: (b, h)
    return pl.pallas_call(
        attend_back_kernel,
        out_shape=(
            jax.ShapeDtypeStruct((tokens, width), LOW),
            jax.ShapeDtypeStruct((2 * tokens, width), LOW),
            jax.ShapeDtypeStruct((2 * tokens, width), LOW),
        ),
        grid_spec=pltpu.PrefetchScalarGridSpec(
            num_scalar_prefetch=1,
            grid=(batches, pairs),
            in_specs=[
                spec(slots, here),
                spec(2 * slots, here),
                spec(2 * slots, lambda b, h, info: (b, h + pairs)),
                spec(slots, here),
                spec(slots, here),
                pl.BlockSpec((1, 1, 8, slots), lambda b, h, info: (b, h, 0, 0)),
            ],
            out_specs=[spec(slots, here), spec(2 * slots, here), spec(2 * slots, here)],
            scratch_shapes=[pltpu.VMEM((slots, slots), F32)],
        ),
        cost_estimate=pl.CostEstimate(
            flops=batches * pairs * 20 * slots * slots * 7 * HD,
            bytes_accessed=24 * tokens * width,
            transcendentals=batches * pairs * 4 * slots * slots,
        ),
        name="attend_back",
    )(info, query, joined, joined, grad, mixed, lse)


def normalize(values):
    center = values - jnp.mean(values, axis=-1, keepdims=True)
    factor = lax.rsqrt(jnp.mean(center * center, axis=-1, keepdims=True) + EPSILON)
    return (center * factor, factor)


def norm_back(grad_normed, normed, factor):
    first = jnp.mean(grad_normed, axis=-1, keepdims=True)
    second = jnp.mean(grad_normed * normed, axis=-1, keepdims=True)
    return factor * (grad_normed - first - normed * second)


def gelu_both(values):
    square = values * values
    bend = jnp.tanh(0.7978845608028654 * (values + 0.044715 * values * square))
    act = 0.5 * values * (1.0 + bend)
    slope = 0.5 * (1.0 + bend) + 0.5 * values * (1.0 - bend * bend) * 0.7978845608028654 * (
        1.0 + 3.0 * 0.044715 * square
    )
    return act, slope


def outer(left, right):
    return lax.dot_general(left, right, (((0,), (0,)), ((), ())), preferred_element_type=F32)


def column_sum(values):
    return jnp.sum(values.astype(F32), axis=0)


def body(
    layer_input,
    lengths,
    out_grad,
    ln1_gain,
    ln1_shift,
    w_qkv,
    b_query,
    b_value,
    w_out,
    b_out,
    ln2_gain,
    ln2_shift,
    w_in,
    b_in,
    w_down,
    b_down,
):
    place = box()
    batches, _, slots, width = layer_input.shape
    tokens = batches * slots
    side = place["yi"]
    rows = w_qkv.shape[0]

    own = layer_input[:, 0]
    early = lax.ppermute(own, "seq", [(0, 1)])

    vectors = jnp.stack([ln1_gain, ln1_shift, b_query, b_value, b_out, ln2_gain, ln2_shift, b_down], 1)
    vectors = jnp.concatenate([vectors, b_in.reshape(rows, -1)], axis=1)
    count = vectors.shape[1]
    vectors = jnp.pad(vectors, ((0, 0), (0, LANES - count)))
    first = gather_z(jnp.concatenate([w_qkv, vectors], axis=1), place)
    cut = 13 * LANES
    left = whole(gather_rest(first[:, :, :cut], "xy", place))
    right = whole(gather_rest(first[:, :, cut:], "yx", place))
    w_out_full = whole(gather_rest(gather_z(w_out, place), "xy", place))
    w_in_full = whole(gather_rest(gather_z(w_in, place), "xy", place))
    w_down_full = whole(gather_rest(gather_z(w_down, place), "yx", place))
    w_q = left[:, :width]
    w_kv = jnp.concatenate([left[:, width:], right[:, : 2 * width - (cut - width)]], axis=1)
    small = right[:, 2 * width - (cut - width) :].T.astype(F32)
    gain1, shift1, bias_q, bias_v, bias_o, gain2, shift2, bias_d = (small[i] for i in range(8))
    bias_in = small[8:count].T.reshape(-1)

    source = jnp.stack([early, own], axis=1).astype(F32)
    normed1, factor1 = normalize(source)
    attn_in = (normed1 * gain1 + shift1).astype(LOW)
    normed1, factor1 = normed1[:, 1].reshape(tokens, width), factor1[:, 1].reshape(tokens, 1)
    source = source[:, 1].reshape(tokens, width)
    attn_own = attn_in[:, 1].reshape(tokens, width)
    attn_all = attn_in.reshape(2 * tokens, width)
    query = (nn(attn_own, w_q) + bias_q).astype(LOW)
    bias_kv = jnp.concatenate([jnp.zeros_like(bias_v), bias_v])
    joined = (nn(attn_all, w_kv) + bias_kv).astype(LOW)
    info = jnp.concatenate([side[None], lengths[:, 0] - side * slots]).astype(jnp.int32)
    mixed, lse = attend(info, query, joined)
    middle = source + nn(mixed, w_out_full) + bias_o

    normed2, factor2 = normalize(middle)
    mlp_in = (normed2 * gain2 + shift2).astype(LOW)
    act, slope = gelu_both(nn(mlp_in, w_in_full) + bias_in)
    act, slope = act.astype(LOW), slope.astype(LOW)
    position = side * slots + jnp.arange(slots, dtype=jnp.int32)
    live = (position[None, :] < lengths).astype(F32).reshape(tokens, 1)
    output = (live * (middle + nn(act, w_down_full) + bias_d)).astype(LOW)

    grad = live * out_grad[:, 0].reshape(tokens, width).astype(F32)
    grad_low = grad.astype(LOW)
    part_down = scatter_core(outer(act, grad_low).astype(LOW), place)
    before = (nt(grad_low, w_down_full) * slope.astype(F32)).astype(LOW)
    part_in = scatter_core(outer(mlp_in, before).astype(LOW), place)
    hidden = nt(before, w_in_full)
    middle_grad = grad + norm_back(hidden * gain2, normed2, factor2)
    attn_grad = middle_grad.astype(LOW)
    part_out = scatter_core(outer(mixed, attn_grad).astype(LOW), place)
    mixed_grad = nt(attn_grad, w_out_full).astype(LOW)
    d_query, d_keys, d_values = attend_back(info, query, joined, mixed_grad, mixed, lse)
    grad_down = scatter_z(scatter_xy(part_down, "yx", place), place)
    grad_in = scatter_z(scatter_xy(part_in, "xy", place), place)
    grad_out = scatter_z(scatter_xy(part_out, "yx", place), place)
    spread = nt(d_keys, w_kv[:, :width]) + nt(d_values, w_kv[:, width:])
    spread = spread.reshape(batches, 2, slots, width)
    returned = lax.ppermute(spread[:, 0].astype(LOW), "seq", [(1, 0)])
    normal = (
        nt(d_query, w_q)
        + spread[:, 1].reshape(tokens, width)
        + returned.reshape(tokens, width).astype(F32)
    )
    input_grad = (middle_grad + norm_back(normal * gain1, normed1, factor1)).astype(LOW)
    sums = jnp.stack(
        [
            jnp.sum(normal * normed1, axis=0),
            jnp.sum(normal, axis=0),
            column_sum(d_query),
            column_sum(d_values),
            column_sum(attn_grad),
            jnp.sum(hidden * normed2, axis=0),
            jnp.sum(hidden, axis=0),
            column_sum(grad_low),
        ],
        axis=1,
    )
    sums = jnp.concatenate([sums, column_sum(before).reshape(width, -1)], axis=1)
    sums = jnp.pad(sums, ((0, 0), (0, LANES - count))).astype(LOW)
    left_grad = outer(attn_own, d_query).astype(LOW)
    key_grad = outer(attn_all, d_keys).astype(LOW)
    value_grad = outer(attn_all, d_values).astype(LOW)
    edge = cut - width
    left_total = jnp.concatenate([left_grad, key_grad[:, :edge]], axis=1)
    right_total = jnp.concatenate([key_grad[:, edge:], value_grad, sums], axis=1)
    left_part = scatter_xy(scatter_core(left_total, place), "yx", place)
    right_part = scatter_xy(scatter_core(right_total, place), "xy", place)
    tail = scatter_z(jnp.concatenate([left_part, right_part], axis=2), place)
    columns = 3 * width
    ends = [tail[:, columns + i] for i in range(8)]
    end_in = tail[:, columns + 8 : columns + count].reshape(-1)
    stacked_out = output.reshape(batches, 1, slots, width)
    stacked_grad = input_grad.reshape(batches, 1, slots, width)
    return (
        stacked_out,
        stacked_grad,
        ends[0],
        ends[1],
        tail[:, :columns],
        ends[2],
        ends[3],
        grad_out,
        ends[4],
        ends[5],
        ends[6],
        grad_in,
        end_in,
        grad_down,
        ends[7],
    )


def solution(mesh):
    vector, matrix = P(("dp", "seq")), P(("dp", "seq"), None)
    sample = P(None, "dp", "seq", None)
    in_specs = (
        sample,
        P(None, "dp"),
        sample,
        vector,
        vector,
        matrix,
        vector,
        vector,
        matrix,
        vector,
        vector,
        vector,
        matrix,
        vector,
        matrix,
        vector,
    )
    out_specs = (
        sample,
        sample,
        vector,
        vector,
        matrix,
        vector,
        vector,
        matrix,
        vector,
        vector,
        vector,
        matrix,
        vector,
        matrix,
        vector,
    )
    return jax.shard_map(body, mesh=mesh, in_specs=in_specs, out_specs=out_specs, check_vma=False)
```
